32 devices in a mesh: row: 8 (over z, x), col: 4 (over y, core).
Axes of the slice: x: 2, y: 2, z: 4, core: 2. Of those that a mesh axis runs over, the one named last changes fastest.
Arguments:
- tokens: bfloat16 [64, 512, 512], P('row', 'col'), may hold values from -6 to 6
- ln1_gain: float32 [512], replicated, may hold values from 0.1 to 1.9
- w_qkv: bfloat16 [512, 1536], replicated
- rel_bias: float32 [16, 49], replicated, may hold values from -4 to 4
- w_proj: bfloat16 [512, 512], replicated, may hold values from -0.25 to 0.25
- ln2_gain: float32 [512], replicated, may hold values from 0.1 to 1.9
- w_up: bfloat16 [512, 2048], replicated, may hold values from -0.25 to 0.25
- w_down: bfloat16 [2048, 512], replicated, may hold values from -0.125 to 0.125
- merge_gain: float32 [2048], replicated, may hold values from 0.3 to 3
- w_merge: bfloat16 [2048, 1024], replicated, may hold values from -0.125 to 0.125
- cotangent: bfloat16 [32, 256, 1024], P('row', 'col'), may hold values from -6 to 6
Outputs:
- merged: bfloat16 [32, 256, 1024], P('row', 'col')
- grad_merge: float32 [2048, 1024], P(('row', 'col'))
- grad_down: float32 [2048, 512], P(('row', 'col'))
The draws below stay inside these ranges and needn't reach their ends.
All inputs are finite; a program needn't handle non-finite values.
Results may differ from the reference program's by a relative error of at most 0.012.
Values may be sent and summed in bfloat16 or wider, within the bound.
A program may use at most 128 MiB of HBM per device.

```python
import math
import jax
import jax.numpy as jnp
from jax import lax

D = 512
HEADS = 16
FF = 2048
H = 64
W = 512


def draw_w_qkv(key, part):
    base = jnp.clip(jax.random.normal(key, (D, 3 * D), jnp.float32), -6.0, 6.0) * D ** (-0.5)
    return base.astype(jnp.bfloat16)


def block_levels(own_key, extent, split, least, high):
    factor_of, own = 1.0, jax.random.fold_in(own_key, 6)
    for axis_at, blocks in split:
        draws = jnp.exp(jax.random.uniform(jax.random.fold_in(own, axis_at), (blocks,), jnp.float32, least / len(split), high / len(split)))
        factor_of = factor_of * jnp.repeat(draws, extent[axis_at] // blocks).reshape([-1 if axis == axis_at else 1 for axis in range(len(extent))])
    return factor_of


def centred(rng, extent, spread, reach, split=(), held_as=jnp.bfloat16):
    array = spread * jax.random.normal(rng, extent, jnp.float32)
    if split:
        array = array * block_levels(rng, extent, split, -0.22, 0.18)
    return jnp.clip(array, -reach, reach).astype(held_as)


def setup_inputs(seed: int = 0) -> dict:
    splits = jax.random.split(jax.random.key(seed), 12)
    tokens = centred(splits[0], (H, W, D), 1.0, 6.0, ((0, 8), (1, 4)))
    ln1_gain = jnp.clip(1.0 + 0.18 * jax.random.normal(splits[1], (D,), jnp.float32), 0.1, 1.9)
    w_qkv = draw_w_qkv(jax.random.fold_in(splits[11], 71), 0)
    rel_bias = centred(splits[3], (HEADS, 49), 1.0, 4.0, (), jnp.float32)
    w_proj = centred(splits[4], (D, D), D ** -0.5, 0.25)
    ln2_gain = jnp.clip(1.0 + 0.18 * jax.random.normal(splits[5], (D,), jnp.float32), 0.1, 1.9)
    w_up = centred(splits[6], (D, FF), D ** -0.5, 0.25)
    w_down = centred(splits[7], (FF, D), FF ** -0.5, 0.125)
    merge_gain = jnp.clip(jnp.exp(jax.random.uniform(splits[8], (4 * D,), jnp.float32, math.log(0.3), math.log(3.0))), 0.3, 3.0)
    w_merge = centred(splits[9], (4 * D, 2 * D), (4 * D) ** -0.5, 0.125)
    cotangent = centred(splits[10], (H // 2, W // 2, 2 * D), 1.0, 6.0, ((0, 8), (1, 4)))
    return dict(tokens=tokens, ln1_gain=ln1_gain, w_qkv=w_qkv, rel_bias=rel_bias, w_proj=w_proj, ln2_gain=ln2_gain, w_up=w_up, w_down=w_down, merge_gain=merge_gain, w_merge=w_merge, cotangent=cotangent)


def layer_norm(value, gain):
    mean = lax.optimization_barrier(jnp.mean(value, axis=-1, keepdims=True))
    var = lax.optimization_barrier(jnp.mean((value - mean) ** 2, axis=-1, keepdims=True))
    return (value - mean) / jnp.sqrt(var + 1e-05) * gain

def reference(tokens, ln1_gain, w_qkv, rel_bias, w_proj, ln2_gain, w_up, w_down, merge_gain, w_merge, cotangent):
    total_rows, total_cols, width = tokens.shape
    heads = rel_bias.shape[0]
    head_dim = width // heads
    normed = layer_norm(tokens.astype(jnp.float32), ln1_gain).astype(jnp.bfloat16)
    flat = normed.reshape(-1, width)
    query = jnp.dot(flat, w_qkv[:, :width], preferred_element_type=jnp.float32).astype(jnp.bfloat16)
    query = query.reshape(total_rows, total_cols, heads, head_dim)
    keyval = jnp.dot(flat, w_qkv[:, width:], preferred_element_type=jnp.float32).astype(jnp.bfloat16)
    keyval = keyval.reshape(total_rows, total_cols, 2, heads, head_dim)
    padded = jnp.pad(keyval, ((3, 3), (3, 3), (0, 0), (0, 0), (0, 0)))
    col_pos = jnp.arange(total_cols)
    bias_t = rel_bias.T
    scale = 1.0 / jnp.sqrt(jnp.float32(head_dim))

    def block(carry, start):
        grad_m, grad_d = carry
        q_blk = lax.dynamic_slice_in_dim(query, start, 2, 0).astype(jnp.float32)
        k_blk = lax.dynamic_slice_in_dim(padded, start, 8, 0)
        row_pos = start + jnp.arange(2)
        scores = []
        masks = []
        for di in range(7):
            for dj in range(7):
                key = k_blk[di:di + 2, dj:dj + total_cols, 0].astype(jnp.float32)
                scores.append(lax.optimization_barrier(jnp.sum(q_blk * key, axis=-1)))
                rows_ok = (row_pos + di - 3 >= 0) & (row_pos + di - 3 < total_rows)
                cols_ok = (col_pos + dj - 3 >= 0) & (col_pos + dj - 3 < total_cols)
                masks.append(rows_ok[:, None] & cols_ok[None, :])
        score = jnp.stack(scores, 0) * scale + bias_t[:, None, None, :]
        valid = jnp.stack(masks, 0)[..., None]
        score = jnp.where(valid, score, -1e+30)
        top = lax.optimization_barrier(jnp.max(score, axis=0, keepdims=True))
        expo = jnp.where(valid, jnp.exp(score - top), 0.0)
        probs = (expo / lax.optimization_barrier(jnp.sum(expo, axis=0, keepdims=True))).astype(jnp.bfloat16)
        attn = jnp.zeros((2, total_cols, heads, head_dim), jnp.float32)
        offset = 0
        for di in range(7):
            for dj in range(7):
                value = k_blk[di:di + 2, dj:dj + total_cols, 1].astype(jnp.float32)
                attn = attn + probs[offset].astype(jnp.float32)[..., None] * value
                offset += 1
        attn = attn.astype(jnp.bfloat16).reshape(-1, width)
        x_blk = lax.dynamic_slice_in_dim(tokens, start, 2, 0).astype(jnp.float32).reshape(-1, width)
        h_one = (x_blk + jnp.dot(attn, w_proj, preferred_element_type=jnp.float32)).astype(jnp.bfloat16)
        normed2 = layer_norm(h_one.astype(jnp.float32), ln2_gain).astype(jnp.bfloat16)
        hidden = jax.nn.gelu(jnp.dot(normed2, w_up, preferred_element_type=jnp.float32), approximate=False).astype(jnp.bfloat16)
        out_y = (h_one.astype(jnp.float32) + jnp.dot(hidden, w_down, preferred_element_type=jnp.float32)).astype(jnp.bfloat16)
        joined = out_y.reshape(1, 2, total_cols // 2, 2, width).transpose(0, 2, 3, 1, 4).reshape(-1, 4 * width).astype(jnp.float32)
        mean = lax.optimization_barrier(jnp.mean(joined, axis=-1, keepdims=True))
        inv = 1.0 / jnp.sqrt(lax.optimization_barrier(jnp.mean((joined - mean) ** 2, axis=-1, keepdims=True)) + 1e-05)
        unit = (joined - mean) * inv
        merge_in = (unit * merge_gain).astype(jnp.bfloat16)
        merged_blk = jnp.dot(merge_in, w_merge, preferred_element_type=jnp.float32).astype(jnp.bfloat16)
        cot = lax.dynamic_slice_in_dim(cotangent, start // 2, 1, 0).reshape(-1, 2 * width)
        grad_m = grad_m + jnp.dot(merge_in.T, cot, preferred_element_type=jnp.float32)
        grad_n = jnp.dot(cot, w_merge.T, preferred_element_type=jnp.float32) * merge_gain
        grad_z = (grad_n - lax.optimization_barrier(jnp.mean(grad_n, axis=-1, keepdims=True)) - unit * lax.optimization_barrier(jnp.mean(grad_n * unit, axis=-1, keepdims=True))) * inv
        grad_y = grad_z.astype(jnp.bfloat16).reshape(1, total_cols // 2, 2, 2, width).transpose(0, 3, 1, 2, 4).reshape(-1, width)
        grad_d = grad_d + jnp.dot(hidden.T, grad_y, preferred_element_type=jnp.float32)
        return ((grad_m, grad_d), merged_blk.reshape(total_cols // 2, 2 * width))
    starts = jnp.arange(0, total_rows, 2).astype(jnp.int32)
    init = (jnp.zeros((4 * width, 2 * width), jnp.float32), jnp.zeros((w_down.shape[0], width), jnp.float32))
    (grad_m, grad_d), merged = lax.scan(block, init, starts)
    count = grad_m.size + grad_d.size
    total = jnp.sum(grad_m * grad_m) + jnp.sum(grad_d * grad_d)
    factor = 1.0 / jnp.sqrt(total / count + 1e-06)
    return (merged, grad_m * factor, grad_d * factor)
```

```python
import jax
import jax.numpy as jnp
from jax import lax
from jax.sharding import PartitionSpec as P


def with_halo(cells, sides, width):
    for axis, dim in sides:
        count = lax.axis_size(axis)
        ends = count - 1
        head = lax.slice_in_dim(cells, 0, width, axis=dim)
        tail = lax.slice_in_dim(cells, cells.shape[dim] - width, cells.shape[dim], axis=dim)
        cells = jnp.concatenate(
            [
                lax.ppermute(tail, axis, [(i, (i + 1) % count) for i in range(ends)]),
                cells,
                lax.ppermute(head, axis, [((i + 1) % count, i) for i in range(ends)]),
            ],
            axis=dim,
        )
    return cells


def layer_norm(value, gain):
    mean = jnp.mean(value, axis=-1, keepdims=True)
    var = jnp.mean((value - mean) ** 2, axis=-1, keepdims=True)
    return (value - mean) / jnp.sqrt(var + 1e-05) * gain


def local(
    tokens,
    ln1_gain,
    w_qkv,
    rel_bias,
    w_proj,
    ln2_gain,
    w_up,
    w_down,
    merge_gain,
    w_merge,
    cotangent,
):
    rows, cols, width = tokens.shape
    heads = rel_bias.shape[0]
    head_dim = width // heads
    x_flat = tokens.astype(jnp.float32).reshape(-1, width)
    normed = layer_norm(x_flat, ln1_gain).astype(jnp.bfloat16)
    query = jnp.dot(normed, w_qkv[:, :width], preferred_element_type=jnp.float32).astype(
        jnp.bfloat16
    )
    query_t = query.reshape(rows, cols, heads, head_dim).transpose(0, 2, 3, 1)
    keyval = jnp.dot(normed, w_qkv[:, width:], preferred_element_type=jnp.float32).astype(
        jnp.bfloat16
    )
    keyval = keyval.reshape(rows, cols, 2 * width).transpose(0, 2, 1)
    padded = with_halo(keyval, (("row", 0), ("col", 2)), 3)
    padded = padded.reshape(rows + 6, 2, heads, head_dim, cols + 6)
    total_rows = rows * lax.axis_size("row")
    total_cols = cols * lax.axis_size("col")
    row_pos = lax.axis_index("row") * rows + jnp.arange(rows)
    col_pos = lax.axis_index("col") * cols + jnp.arange(cols)
    scores = []
    masks = []
    for di in range(7):
        for dj in range(7):
            key = padded[di : di + rows, 0, :, :, dj : dj + cols]
            scores.append(
                jnp.einsum("rhdc,rhdc->rhc", query_t, key, preferred_element_type=jnp.float32)
            )
            rows_ok = (row_pos + di - 3 >= 0) & (row_pos + di - 3 < total_rows)
            cols_ok = (col_pos + dj - 3 >= 0) & (col_pos + dj - 3 < total_cols)
            masks.append(rows_ok[:, None] & cols_ok[None, :])
    scale = 1.0 / jnp.sqrt(jnp.float32(head_dim))
    score = jnp.stack(scores, 0) * scale + rel_bias.T[:, None, :, None]
    valid = jnp.stack(masks, 0)[:, :, None, :]
    score = jnp.where(valid, score, -1e30)
    top = jnp.max(score, axis=0, keepdims=True)
    expo = jnp.where(valid, jnp.exp(score - top), 0.0)
    probs = (expo / jnp.sum(expo, axis=0, keepdims=True)).astype(jnp.bfloat16)
    attn = jnp.zeros((rows, heads, head_dim, cols), jnp.float32)
    offset = 0
    for di in range(7):
        for dj in range(7):
            value = padded[di : di + rows, 1, :, :, dj : dj + cols]
            attn = attn + jnp.einsum(
                "rhc,rhdc->rhdc", probs[offset], value, preferred_element_type=jnp.float32
            )
            offset += 1
    attn = attn.astype(jnp.bfloat16).transpose(0, 3, 1, 2).reshape(-1, width)
    h_one = (x_flat + jnp.dot(attn, w_proj, preferred_element_type=jnp.float32)).astype(
        jnp.bfloat16
    )
    normed2 = layer_norm(h_one.astype(jnp.float32), ln2_gain).astype(jnp.bfloat16)
    hidden = jax.nn.gelu(
        jnp.dot(normed2, w_up, preferred_element_type=jnp.float32), approximate=False
    ).astype(jnp.bfloat16)
    out_y = (
        h_one.astype(jnp.float32) + jnp.dot(hidden, w_down, preferred_element_type=jnp.float32)
    ).astype(jnp.bfloat16)
    joined = (
        out_y.reshape(rows // 2, 2, cols // 2, 2, width)
        .transpose(0, 2, 3, 1, 4)
        .reshape(-1, 4 * width)
        .astype(jnp.float32)
    )
    mean = jnp.mean(joined, axis=-1, keepdims=True)
    inv = 1.0 / jnp.sqrt(jnp.mean((joined - mean) ** 2, axis=-1, keepdims=True) + 1e-05)
    unit = (joined - mean) * inv
    merge_in = (unit * merge_gain).astype(jnp.bfloat16)
    merged = jnp.dot(merge_in, w_merge, preferred_element_type=jnp.float32).astype(jnp.bfloat16)
    merged = merged.reshape(rows // 2, cols // 2, 2 * width)
    cot = cotangent.reshape(-1, 2 * width)
    grad_m = jnp.dot(merge_in.T, cot, preferred_element_type=jnp.float32)
    grad_n = jnp.dot(cot, w_merge.T, preferred_element_type=jnp.float32) * merge_gain
    grad_z = (
        grad_n
        - jnp.mean(grad_n, axis=-1, keepdims=True)
        - unit * jnp.mean(grad_n * unit, axis=-1, keepdims=True)
    ) * inv
    grad_y = (
        grad_z.astype(jnp.bfloat16)
        .reshape(rows // 2, cols // 2, 2, 2, width)
        .transpose(0, 3, 1, 2, 4)
        .reshape(-1, width)
    )
    grad_d = jnp.dot(hidden.T, grad_y, preferred_element_type=jnp.float32)
    count = grad_m.size + grad_d.size
    both = jnp.concatenate([grad_m.astype(jnp.bfloat16), grad_d.astype(jnp.bfloat16)], axis=1)
    share = lax.psum_scatter(both, ("row", "col"), scatter_dimension=0, tiled=True).astype(
        jnp.float32
    )
    total = lax.psum(jnp.sum(share * share), ("row", "col"))
    share_m, share_d = share[:, : grad_m.shape[1]], share[:, grad_m.shape[1] :]
    factor = 1.0 / jnp.sqrt(total / count + 1e-06)
    return (merged, share_m * factor, share_d * factor)


def solution(mesh):
    placed = (
        P("row", "col", None),
        P(),
        P(),
        P(),
        P(),
        P(),
        P(),
        P(),
        P(),
        P(),
        P("row", "col", None),
    )
    return jax.shard_map(
        local,
        mesh=mesh,
        in_specs=placed,
        out_specs=(P("row", "col", None), P(("row", "col"), None), P(("row", "col"), None)),
        check_vma=False,
    )
```

```python
import functools

import jax
import jax.numpy as jnp
from jax import lax
from jax.experimental import pallas as pl
from jax.experimental.pallas import tpu as pltpu
from jax.sharding import PartitionSpec as P

F32 = jnp.float32
BF16 = jnp.bfloat16
REACH = 3
SPAN = 2 * REACH + 1
TILE = 8
LEAD = 4
LOW = -1e30


def shifted(cells, axis, dim, width):
    count = lax.axis_size(axis)
    ends = count - 1
    size = cells.shape[dim]
    head = lax.slice_in_dim(cells, 0, width, axis=dim)
    tail = lax.slice_in_dim(cells, size - width, size, axis=dim)
    before = lax.ppermute(tail, axis, [(i, (i + 1) % count) for i in range(ends)])
    after = lax.ppermute(head, axis, [((i + 1) % count, i) for i in range(ends)])
    return before, after


def cost(flops, *arrays):
    return pl.CostEstimate(
        flops=flops,
        bytes_accessed=sum(a.size * a.dtype.itemsize for a in arrays),
        transcendentals=0,
    )


def normalise(value):
    mean = jnp.mean(value, axis=-1, keepdims=True)
    value = value - mean
    inv = 1.0 / jnp.sqrt(jnp.mean(value * value, axis=-1, keepdims=True) + 1e-05)
    return value * inv, inv


def dot(a, b, dims=((1,), (0,))):
    return lax.dot_general(a, b, (dims, ((), ())), preferred_element_type=F32)


def query_kernel(x_ref, gain_ref, w_ref, out_ref):
    unit, _ = normalise(x_ref[...].astype(F32))
    out_ref[...] = dot((unit * gain_ref[...]).astype(BF16), w_ref[...]).astype(BF16)


def back_kernel(cot_ref, w_ref, gain_ref, out_ref):
    out_ref[...] = dot(cot_ref[...], w_ref[...], ((1,), (1,))) * gain_ref[...]


def attend_kernel(
    heads, head_dim, x_ref, gain_ref, w_ref, q_ref, tab_ref, edge_ref, out_ref, kv_ref
):
    step = pl.program_id(0)
    width = gain_ref.shape[1]
    rows, span, _ = x_ref.shape
    block = rows * span
    unit, _ = normalise(x_ref[...].astype(F32).reshape(block, width))
    fresh = dot((unit * gain_ref[...]).astype(BF16), w_ref[...]).astype(BF16)
    kv_ref[:block, :] = kv_ref[block:, :]
    kv_ref[block:, :] = fresh

    @pl.when(step > 0)
    def _():
        groups = tab_ref.shape[0]
        each = width // groups
        per = heads // groups
        count = q_ref.shape[0]
        lane = lax.broadcasted_iota(jnp.int32, (1, each), 1)
        for g in range(groups):
            q = q_ref[:, g * each : (g + 1) * each]
            stacked = jnp.concatenate(
                [
                    jnp.where((lane >= h * head_dim) & (lane < (h + 1) * head_dim), q, jnp.zeros_like(q))
                    for h in range(per)
                ],
                axis=0,
            )
            key = kv_ref[:, g * each : (g + 1) * each]
            value = kv_ref[:, width + g * each : width + (g + 1) * each]
            score = dot(stacked, key, ((1,), (1,))) * (head_dim**-0.5)
            score = score + tab_ref[g] + edge_ref[0]
            top = jnp.max(score, axis=-1, keepdims=True)
            expo = jnp.exp(score - top)
            total = jnp.sum(expo, axis=-1, keepdims=True)
            probs = (expo * (1.0 / total)).astype(BF16)
            mixed = dot(probs, value)
            acc = jnp.zeros((count, each), F32)
            for h in range(per):
                part = mixed[h * count : (h + 1) * count]
                acc = jnp.where((lane >= h * head_dim) & (lane < (h + 1) * head_dim), part, acc)
            out_ref[:, g * each : (g + 1) * each] = acc.astype(BF16)


def mlp_kernel(
    sub, a_ref, x_ref, gain_ref, wp_ref, wu_ref, wd_ref, hid_ref, z_ref
):
    width = x_ref.shape[1]
    h_one = (x_ref[...].astype(F32) + dot(a_ref[...], wp_ref[...])).astype(BF16)
    unit, _ = normalise(h_one.astype(F32))
    normed = (unit * gain_ref[...]).astype(BF16)
    y = h_one.astype(F32)
    piece = 512
    for c in range(0, wu_ref.shape[1], piece):
        up = dot(normed, wu_ref[:, c : c + piece])
        hid = (0.5 * up * (1.0 + lax.erf(up * (0.5**0.5)))).astype(BF16)
        hid_ref[:, c : c + piece] = hid
        y = y + dot(hid, wd_ref[c : c + piece, :])
    y = y.astype(BF16)
    tiles = y.shape[0] // (4 * sub)
    for t in range(tiles):
        for p in range(4):
            at = (4 * t + p) * sub
            z_ref[t * sub : (t + 1) * sub, p * width : (p + 1) * width] = y[at : at + sub]


def grad_kernel(
    sub, z_ref, hid_ref, gn_ref, cot_ref, gain_ref, wm_ref, merged_ref, grad_ref, m_ref, dy_ref
):
    merged_tokens, wide = z_ref.shape
    width = wide // 4
    out_w = cot_ref.shape[1]
    chunk = 4 * sub

    @pl.loop(0, merged_tokens // chunk)
    def _(c):
        at = pl.ds(pl.multiple_of(c * chunk, chunk), chunk)
        unit, inv = normalise(z_ref[at, :].astype(F32))
        m_ref[at, :] = (unit * gain_ref[...]).astype(BF16)
        gn = gn_ref[at, :]
        gn = gn - jnp.mean(gn, axis=-1, keepdims=True) - unit * jnp.mean(
            gn * unit, axis=-1, keepdims=True
        )
        dz = (gn * inv).astype(BF16)
        for t in range(chunk // sub):
            for p in range(4):
                to = pl.multiple_of(c * (4 * chunk), 4 * chunk) + (4 * t + p) * sub
                dy_ref[pl.ds(to, sub), :] = dz[
                    t * sub : (t + 1) * sub, p * width : (p + 1) * width
                ]

    piece = 256

    @pl.loop(0, out_w // piece)
    def _(c):
        at = pl.ds(pl.multiple_of(c * piece, piece), piece)
        merged_ref[:, at] = dot(m_ref[...], wm_ref[:, at]).astype(BF16)

    @pl.loop(0, wide // piece)
    def _(c):
        at = pl.ds(pl.multiple_of(c * piece, piece), piece)
        grad_m = dot(m_ref[:, at], cot_ref[...], ((0,), (0,))).astype(BF16)
        for p in range(out_w // width):
            grad_ref[p, at, :] = grad_m[:, p * width : (p + 1) * width]
        grad_ref[out_w // width, at, :] = dot(
            hid_ref[:, at], dy_ref[...], ((0,), (0,))
        ).astype(BF16)


def place(dims, at, value):
    return tuple(value if d == at else slice(None) for d in dims)


def reduce_kernel(bits, orders, size, in_ref, om_ref, od_ref, *scratch):
    steps, parts = len(bits), len(orders)
    recv, scratch = scratch[:steps], scratch[steps:]
    work, scratch = scratch[: steps - 1], scratch[steps - 1 :]
    acc, v_send, v_recv, send_sem, recv_sem, vs_sem, vr_sem = scratch
    mine, peer = {}, {}
    for axis, weight in bits:
        here = lax.axis_index(axis)
        bit = (here // weight) % 2
        mine[axis, weight] = bit
        peer[axis, weight] = {axis: here + weight * (1 - 2 * bit)}

    barrier = pltpu.get_barrier_semaphore()
    for bit in bits:
        pl.semaphore_signal(
            barrier, inc=1, device_id=peer[bit], device_id_type=pl.DeviceIdType.MESH
        )
    pl.semaphore_wait(barrier, steps)

    def held(k, p):
        return [b for b in bits if b not in orders[p][:k]]

    def exchange(k, p):
        bit = orders[p][k]
        source = in_ref if k == 0 else work[k - 1]
        return pltpu.make_async_remote_copy(
            src_ref=source.at[(p,) + place(held(k, p), bit, 1 - mine[bit])],
            dst_ref=recv[k].at[p],
            send_sem=send_sem.at[k, p],
            recv_sem=recv_sem.at[k, p],
            device_id=peer[bit],
            device_id_type=pl.DeviceIdType.MESH,
        )

    flying = [exchange(0, p) for p in range(parts)]
    for copy in flying:
        copy.start()
    for k in range(steps):
        for p in range(parts):
            flying[p].wait()
            bit = orders[p][k]
            source = in_ref if k == 0 else work[k - 1]
            dims = held(k, p)
            left = [d for d in dims if d != bit]

            @pl.loop(0, 2 ** len(left))
            def _(j):
                digits = [(j // 2 ** (len(left) - 1 - n)) % 2 for n in range(len(left))]
                chosen = dict(zip(left, digits))
                own = tuple(mine[bit] if d == bit else chosen[d] for d in dims)
                value = source[(p,) + own].astype(F32) + recv[k][(p,) + tuple(digits)].astype(F32)
                if k < steps - 1:
                    work[k][(p,) + tuple(digits)] = value.astype(BF16)
                else:
                    acc[p] = value

            if k < steps - 1:
                flying[p] = exchange(k + 1, p)
                flying[p].start()

    total = jnp.zeros(v_send.shape[1:], F32)
    for p in range(parts):
        square = acc[p] * acc[p]
        for r in range(0, square.shape[0], 8):
            for c in range(0, square.shape[1], 128):
                total = total + square[r : r + 8, c : c + 128]
    for k, bit in enumerate(bits):
        v_send[k] = total
        copy = pltpu.make_async_remote_copy(
            src_ref=v_send.at[k],
            dst_ref=v_recv.at[k],
            send_sem=vs_sem.at[k],
            recv_sem=vr_sem.at[k],
            device_id=peer[bit],
            device_id_type=pl.DeviceIdType.MESH,
        )
        copy.start()
        copy.wait()
        total = total + v_recv[k]
    total = jnp.sum(jnp.sum(total, axis=0, keepdims=True), axis=1, keepdims=True)
    factor = 1.0 / jnp.sqrt(total / size + 1e-06)
    wide = od_ref.shape[1]
    for p in range(parts - 1):
        om_ref[:, p * wide : (p + 1) * wide] = acc[p] * factor
    od_ref[...] = acc[parts - 1] * factor


def reduce_grads(both):
    parts, tall, wide = both.shape
    bits = []
    for axis in ("row", "col"):
        weight = lax.axis_size(axis) // 2
        while weight:
            bits.append((axis, weight))
            weight //= 2
    steps = len(bits)
    first = [b for b in bits if b == ("col", 1)]
    swap = [b for b in (("row", 1), ("col", 2), ("row", 2)) if b in bits]
    rest = [b for b in bits[::-1] if b not in first and b not in swap]
    orders = []
    for p in range(parts):
        turn = p % max(1, len(swap))
        orders.append(tuple(first + swap[turn:] + swap[:turn] + rest))
    rows = tall // 2**steps
    shapes = [(parts,) + (2,) * (steps - 1 - k) + (rows, wide) for k in range(steps)]
    vector = pltpu.VMEM((steps, 8, 128), F32)
    return pl.pallas_call(
        functools.partial(reduce_kernel, tuple(bits), tuple(orders), both.size),
        in_specs=[pl.BlockSpec(memory_space=pltpu.VMEM)],
        out_specs=[pl.BlockSpec(memory_space=pltpu.VMEM)] * 2,
        out_shape=[
            jax.ShapeDtypeStruct((rows, (parts - 1) * wide), F32),
            jax.ShapeDtypeStruct((rows, wide), F32),
        ],
        scratch_shapes=[pltpu.VMEM(s, BF16) for s in shapes]
        + [pltpu.VMEM(s, BF16) for s in shapes[:-1]]
        + [
            pltpu.VMEM((parts, rows, wide), F32),
            vector,
            vector,
            pltpu.SemaphoreType.DMA((steps, parts)),
            pltpu.SemaphoreType.DMA((steps, parts)),
            pltpu.SemaphoreType.DMA((steps,)),
            pltpu.SemaphoreType.DMA((steps,)),
        ],
        compiler_params=pltpu.CompilerParams(
            collective_id=0, has_side_effects=True, vmem_limit_bytes=56 * 2**20
        ),
        name="reduce",
    )(both.reshape((parts,) + (2,) * steps + (rows, wide)))


def local(
    tokens,
    ln1_gain,
    w_qkv,
    rel_bias,
    w_proj,
    ln2_gain,
    w_up,
    w_down,
    merge_gain,
    w_merge,
    cotangent,
):
    rows, cols, width = tokens.shape
    heads = rel_bias.shape[0]
    head_dim = width // heads
    ff = w_up.shape[1]
    tiles = cols // TILE
    blocks = tiles + 1
    held = rows * TILE
    sub = held // 4
    near = (rows + 2 * REACH) * TILE
    count = rows * cols
    merged_count = count // 4
    params = pltpu.CompilerParams(vmem_limit_bytes=56 * 2**20)

    above, below = shifted(tokens, "row", 0, REACH)
    mine = (
        tokens.reshape(rows // 2, 2, tiles, TILE // 2, 2, width)
        .transpose(2, 4, 1, 0, 3, 5)
        .reshape(count, width)
    )
    cot = (
        cotangent.reshape(rows // 2, tiles, TILE // 2, 2 * width)
        .transpose(1, 0, 2, 3)
        .reshape(merged_count, 2 * width)
    )
    gain1 = ln1_gain[None, :]
    gain2 = ln2_gain[None, :]
    gain_m = merge_gain[None, :]

    step = count // 4
    query = pl.pallas_call(
        query_kernel,
        grid=(4,),
        in_specs=[
            pl.BlockSpec((step, width), lambda i: (i, 0)),
            pl.BlockSpec((1, width), lambda i: (0, 0)),
            pl.BlockSpec((width, width), lambda i: (0, 0)),
        ],
        out_specs=pl.BlockSpec((step, width), lambda i: (i, 0)),
        out_shape=jax.ShapeDtypeStruct((count, width), BF16),
        cost_estimate=cost(2 * count * width * width, mine, mine),
        name="query",
    )(mine, gain1, w_qkv)
    back = pl.pallas_call(
        back_kernel,
        grid=(4,),
        in_specs=[
            pl.BlockSpec((merged_count, 2 * width), lambda i: (0, 0)),
            pl.BlockSpec((width, 2 * width), lambda i: (i, 0)),
            pl.BlockSpec((1, width), lambda i: (0, i)),
        ],
        out_specs=pl.BlockSpec((merged_count, width), lambda i: (0, i)),
        out_shape=jax.ShapeDtypeStruct((merged_count, 4 * width), F32),
        cost_estimate=cost(16 * merged_count * width * width, cot, w_merge),
        name="back",
    )(cot, w_merge, gain_m)

    q_at = jnp.arange(held)
    q_col = q_at % (TILE // 2) * 2 + q_at // (2 * sub)
    q_row = q_at % sub // (TILE // 2) * 2 + q_at // sub % 2
    k_at = jnp.arange(2 * near)
    k_row = k_at % near // TILE
    k_col = k_at // near * TILE + k_at % TILE
    d_row = k_row[None, :] - q_row[:, None]
    d_col = k_col[None, :] - q_col[:, None] + (REACH - LEAD)
    inside = (d_row >= 0) & (d_row < SPAN) & (d_col >= 0) & (d_col < SPAN)
    where = jnp.where(inside, d_row * SPAN + d_col, -1)
    hot = (where[None] == jnp.arange(SPAN * SPAN)[:, None, None]).astype(F32)
    table = jnp.einsum("ho,oqk->hqk", rel_bias, hot, precision=lax.Precision.HIGHEST)
    groups = max(1, width // 256)
    table = jnp.where(inside, table, LOW).reshape(groups, heads // groups * held, 2 * near)
    total_rows = rows * lax.axis_size("row")
    total_cols = cols * lax.axis_size("col")
    at_row = lax.axis_index("row") * rows + k_row - REACH
    at_col = (
        lax.axis_index("col") * cols + (k_col - LEAD)[None, :] + TILE * jnp.arange(tiles)[:, None]
    )
    on_grid = (at_row >= 0) & (at_row < total_rows) & (at_col >= 0) & (at_col < total_cols)
    edge = jnp.where(on_grid, 0.0, LOW).astype(F32)[:, None, :]

    tall = jnp.concatenate([above, tokens, below], axis=0)
    left, right = shifted(tall, "col", 1, LEAD)
    padded = jnp.concatenate([left, tall, right], axis=1)

    last = lambda i: (jnp.maximum(i - 1, 0), 0)
    fixed2 = lambda i: (0, 0)
    attn = pl.pallas_call(
        functools.partial(attend_kernel, heads, head_dim),
        grid=(blocks,),
        in_specs=[
            pl.BlockSpec((rows + 2 * REACH, TILE, width), lambda i: (0, i, 0)),
            pl.BlockSpec((1, width), fixed2),
            pl.BlockSpec((width, 2 * width), fixed2),
            pl.BlockSpec((held, width), last),
            pl.BlockSpec(table.shape, lambda i: (0, 0, 0)),
            pl.BlockSpec((1, 1, 2 * near), lambda i: (jnp.maximum(i - 1, 0), 0, 0)),
        ],
        out_specs=pl.BlockSpec((held, width), last),
        out_shape=jax.ShapeDtypeStruct((count, width), BF16),
        scratch_shapes=[pltpu.VMEM((2 * near, 2 * width), BF16)],
        compiler_params=params,
        cost_estimate=cost(8 * count * 2 * width * width, padded, table),
        name="attend",
    )(padded, gain1, w_qkv[:, width:], query, table, edge)

    hidden, z = pl.pallas_call(
        functools.partial(mlp_kernel, sub),
        grid=(4,),
        in_specs=[
            pl.BlockSpec((step, width), lambda i: (i, 0)),
            pl.BlockSpec((step, width), lambda i: (i, 0)),
            pl.BlockSpec((1, width), fixed2),
            pl.BlockSpec((width, width), fixed2),
            pl.BlockSpec((width, ff), fixed2),
            pl.BlockSpec((ff, width), fixed2),
        ],
        out_specs=[
            pl.BlockSpec((step, ff), lambda i: (i, 0)),
            pl.BlockSpec((step // 4, 4 * width), lambda i: (i, 0)),
        ],
        out_shape=[
            jax.ShapeDtypeStruct((count, ff), BF16),
            jax.ShapeDtypeStruct((merged_count, 4 * width), BF16),
        ],
        compiler_params=params,
        cost_estimate=cost(4 * count * ff * width, w_up, w_down),
        name="mlp",
    )(attn, mine, gain2, w_proj, w_up, w_down)

    merged, both = pl.pallas_call(
        functools.partial(grad_kernel, sub),
        in_specs=[pl.BlockSpec(memory_space=pltpu.VMEM)] * 6,
        out_specs=[pl.BlockSpec(memory_space=pltpu.VMEM)] * 2,
        out_shape=[
            jax.ShapeDtypeStruct((merged_count, 2 * width), BF16),
            jax.ShapeDtypeStruct((3, 4 * width, width), BF16),
        ],
        scratch_shapes=[
            pltpu.VMEM((merged_count, 4 * width), BF16),
            pltpu.VMEM((count, width), BF16),
        ],
        compiler_params=params,
        cost_estimate=cost(2 * count * ff * width, hidden),
        name="grads",
    )(z, hidden, back, cot, gain_m, w_merge)

    merged = (
        merged.reshape(tiles, rows // 2, TILE // 2, 2 * width)
        .transpose(1, 0, 2, 3)
        .reshape(rows // 2, cols // 2, 2 * width)
    )
    grad_merge, grad_down = reduce_grads(both)
    return (merged, grad_merge, grad_down)


def solution(mesh):
    placed = (
        P("row", "col", None),
        P(),
        P(),
        P(),
        P(),
        P(),
        P(),
        P(),
        P(),
        P(),
        P("row", "col", None),
    )
    return jax.shard_map(
        local,
        mesh=mesh,
        in_specs=placed,
        out_specs=(P("row", "col", None), P(("row", "col"), None), P(("row", "col"), None)),
        check_vma=False,
    )
```
